256 devices in a mesh: row: 8 (over z), col: 16 (over x, y), grid: 2 (over core).
Axes of the slice: x: 4, y: 4, z: 8, core: 2. Of those that a mesh axis runs over, the one named last changes fastest.
Arguments:
- density: bfloat16 [2, 8, 4, 128, 2048], P(None, 'row', None, 'grid', 'col'), may hold values from -0.01171875 to 0.01171875
- basis_values: bfloat16 [128, 256, 512], P(('row', 'col'), 'grid'), may hold values from -6 to 6
- quad_weight: float32 [128, 256], P(('row', 'col'), 'grid'), may hold values from 0.01 to 0.1
- screen: int32 [128, 256], P(('row', 'col'), 'grid'), may hold values 0 or 1
- tile_list: int32 [128, 4], replicated, may hold values from 0 to 15, as said below
Outputs:
- potential_first: bfloat16 [2, 8, 4, 128, 2048], P(None, 'row', None, 'grid', 'col')
- potential_second: bfloat16 [2, 8, 4, 128, 2048], P(None, 'row', None, 'grid', 'col')
The draws below stay inside these ranges and needn't reach their ends.
Inputs may be any that keep to these rules, and one draw needn't show every extreme that they name: `tile_list`: the 4 tile indices of a batch have distinct remainders modulo 8.
All inputs are finite; a program needn't handle non-finite values. No bound on the sum of `screen` on one device may be relied on, other than what follows from the above.
Results may differ from the reference program's by a relative error of at most 0.014.
Values may be sent and summed in bfloat16 or wider, within the bound.
No kernel may reach another device: no remote copies, remote signals or barrier semaphores. Data moves between devices by JAX's collectives and lax.ppermute only.
A program may use at most 64 MiB of HBM per device.

```python
import math
import jax
import jax.numpy as jnp
from jax import lax

TILE = 128
TB = 4
RT = 2
PTS = 256
ROW_GROUPS = 8
NT = 16
BATCHES = 128
N_GRID = 2


def draw_tile_list(key, part):
    residues = NT // RT
    row_keys = jax.random.split(jax.random.fold_in(key, 11), BATCHES)
    picked = jax.vmap(lambda single: jax.random.permutation(single, residues)[:TB])(row_keys)
    multiple = jax.random.randint(jax.random.fold_in(key, 12), (BATCHES, TB), 0, RT)
    return (multiple * residues + picked).astype(jnp.int32)


def plant(result, key, smallest, top_value):
    shape = result.shape
    place = [jax.random.randint(jax.random.fold_in(key, axis), (), 0, shape[axis]) for axis in range(len(shape))]
    result = result.at[tuple(place)].set(smallest)
    longest = shape.index(max(shape))
    place[longest] = (place[longest] + 1) % shape[longest]
    return result.at[tuple(place)].set(top_value)


def levels(own_key, extent, pieces, low, largest):
    def one(dim, shards_of):
        heights = jax.random.uniform(jax.random.fold_in(jax.random.fold_in(own_key, 6), dim), (shards_of,), jnp.float32, low / len(pieces), largest / len(pieces))
        return jnp.repeat(jnp.exp(heights), extent[dim] // shards_of).reshape((-1,) + (1,) * (len(extent) - dim - 1))

    factor_of = one(*pieces[0])
    for cut in pieces[1:]:
        factor_of = factor_of * one(*cut)
    return factor_of


def noise(rng, extent, deviation, most, shards=(), kind=jnp.bfloat16):
    array = jax.random.normal(rng, extent, jnp.float32) * deviation
    if len(shards) > 0:
        array = levels(rng, extent, shards, -0.22, 0.18) * array
    return jnp.clip(array, min=-most, max=most).astype(kind)


def setup_inputs(seed: int = 0) -> dict:
    streams_of = jax.random.split(jax.random.key(seed), 6)
    density = noise(streams_of[0], (RT, ROW_GROUPS, 4, TILE, NT * TILE), ((TB * TILE) ** 2) ** -0.5, 0.01171875, ((1, 8), (3, 2), (4, 16)))
    basis_values = noise(streams_of[1], (BATCHES, PTS, TB * TILE), 1.0, 6.0, ((0, 128), (1, 2)))
    quad_weight = jnp.clip(jnp.exp(math.log(0.1) - 2.3025851 * jax.random.uniform(streams_of[2], (BATCHES, PTS), jnp.float32) ** levels(streams_of[2], (BATCHES, PTS), ((0, 128), (1, 2)), -0.2, 0.2)), 0.01, 0.1)
    screen = plant((jax.random.randint(streams_of[3], (BATCHES, PTS), 0, 4) < 3).astype(jnp.int32), jax.random.fold_in(streams_of[3], 1), 0, 1)
    tile_list = draw_tile_list(jax.random.fold_in(streams_of[5], 71), 0)
    return dict(density=density, basis_values=basis_values, quad_weight=quad_weight, screen=screen, tile_list=tile_list)


MIXING = 0.001

def local_potential(densities):
    total_density = densities[:, 0:1]
    spin_density = densities[:, 1:4]
    first_part = total_density / jnp.sqrt(1.0 + total_density * total_density)
    spin_norm = jnp.sqrt(1.0 + lax.optimization_barrier(jnp.sum(spin_density * spin_density, axis=1, keepdims=True)))
    return jnp.concatenate([first_part, spin_density / spin_norm], axis=1)

def build(density, basis_values, point_weight, tile_list):
    row_tiles, n_row, components, tile_width, width = density.shape
    n_tiles = width // tile_width
    tiles = density.reshape(row_tiles * n_row, components, tile_width, n_tiles, tile_width)
    n_col = basis_values.shape[0] // n_row
    half_points = basis_values.shape[1] // N_GRID
    per_batch = tile_list.shape[1]
    span = per_batch * tile_width

    def batch_potential(batch):
        batch_list = tile_list[batch]
        picked = jnp.take(jnp.take(tiles, batch_list, axis=0), batch_list, axis=3)
        dens_block = picked.transpose(0, 2, 1, 3, 4).reshape(span, components * span)
        samples = basis_values[batch]
        contracted = jnp.dot(samples, dens_block, preferred_element_type=jnp.float32)
        densities = lax.optimization_barrier(jnp.sum(contracted.reshape(-1, components, span) * samples.astype(jnp.float32)[:, None, :], axis=2))
        potential_scale = point_weight[batch][:, None] * local_potential(densities)
        weighted = (samples.astype(jnp.float32)[:, None, :] * potential_scale[:, :, None]).astype(jnp.bfloat16)
        weighted = weighted.reshape(-1, components * span)
        combined = jnp.zeros((span, components * span), jnp.float32)
        for member in range(N_GRID):
            lower = member * half_points
            partial_value = lax.dot_general(samples[lower:lower + half_points], weighted[lower:lower + half_points], (((0,), (0,)), ((), ())), preferred_element_type=jnp.float32)
            combined = combined + partial_value.astype(jnp.bfloat16).astype(jnp.float32)
        return combined

    def column_pass(total, column):

        def row_pass(accum, row_index):
            batch = row_index * n_col + column
            batch_list = tile_list[batch]
            slab = batch_potential(batch).reshape(per_batch, tile_width, components, per_batch, tile_width)
            slab = slab.transpose(0, 3, 2, 1, 4)
            accum = accum.at[batch_list[:, None], :, :, batch_list[None, :], :].add(slab)
            return (accum, None)
        start = jnp.zeros((n_tiles, components, tile_width, n_tiles, tile_width), jnp.float32)
        accum, ignored = lax.scan(row_pass, start, jnp.arange(n_row, dtype=jnp.int32))
        return (total + accum.astype(jnp.bfloat16).astype(jnp.float32), None)
    total_start = jnp.zeros((n_tiles, components, tile_width, n_tiles, tile_width), jnp.float32)
    total, ignored = lax.scan(column_pass, total_start, jnp.arange(n_col, dtype=jnp.int32))
    return total.astype(jnp.bfloat16).reshape(row_tiles, n_row, components, tile_width, width)

def reference(density, basis_values, quad_weight, screen, tile_list):
    point_weight = quad_weight * screen.astype(jnp.float32)
    potential_first = build(density, basis_values, point_weight, tile_list)
    updated = (density.astype(jnp.float32) + MIXING * potential_first.astype(jnp.float32)).astype(jnp.bfloat16)
    potential_second = build(updated, basis_values, point_weight, tile_list)
    return (potential_first, potential_second)
```

```python
import functools

import jax
import jax.numpy as jnp
from jax import lax
from jax.experimental import pallas as pl
from jax.experimental.pallas import tpu as pltpu
from jax.sharding import PartitionSpec as P

MIXING = 0.001
VMEM_BYTES = 32 * 1024 * 1024


def everyone(x, n):
    return jnp.broadcast_to(x[None], (n, *x.shape))


def find(tile_list, batch, n_row, my_row):
    columns = [tile_list[batch, s] for s in range(tile_list.shape[1])]
    slot = jnp.int32(0)
    multiple = jnp.int32(0)
    present = jnp.bool_(False)
    for s, tile in enumerate(columns):
        match = lax.rem(tile, n_row) == my_row
        slot = jnp.where(match, s, slot)
        multiple = jnp.where(match, lax.div(tile, n_row), multiple)
        present = jnp.logical_or(present, match)
    return columns, slot, multiple, present


def own_rows(basis, slot, half, tile_width, half_tile):
    points = basis.shape[0] * basis.shape[2]
    block = basis[:, 0, :, pl.ds(pl.multiple_of(slot * tile_width, tile_width), tile_width)]
    block = block.reshape(points, tile_width)
    rows = lax.broadcasted_iota(jnp.int32, (half_tile, tile_width), 0) + half * half_tile
    lanes = lax.broadcasted_iota(jnp.int32, (half_tile, tile_width), 1)
    chosen = jnp.where(rows == lanes, 1.0, 0.0).astype(jnp.bfloat16)
    return lax.dot_general(chosen, block, (((1,), (1,)), ((), ())), preferred_element_type=jnp.float32)


def density_kernel(tile_list, strip, basis, weight, screen, out, block, sums, *, n_row, n_col, comps, half_tile, width):
    step = pl.program_id(0)
    my_row = lax.axis_index("row")
    my_col = lax.axis_index("col")
    half = lax.axis_index("grid")
    span = comps * half_tile
    points = basis.shape[0] * basis.shape[2]

    @pl.when(step == 0)
    def _():
        sums[...] = jnp.zeros_like(sums)
        own = weight[...] * screen[...].astype(jnp.float32)
        sums[comps, 0:1, 0 : own.shape[1]] = own

    columns, slot, multiple, present = find(tile_list, step * n_col + my_col, n_row, my_row)

    @pl.when(present)
    def _():
        for s, tile in enumerate(columns):
            first = pl.multiple_of(multiple * span, span)
            block[:, s * width : (s + 1) * width] = strip[tile, pl.ds(first, span), :]
        samples = basis[:, 0].reshape(points, basis.shape[3])
        part = lax.dot_general(
            block[...], samples, (((1,), (1,)), ((), ())), preferred_element_type=jnp.float32
        )
        rows = own_rows(basis, slot, half, width, half_tile)
        for comp in range(comps):
            piece = part[comp * half_tile : (comp + 1) * half_tile, :] * rows
            sums[comp, pl.ds(step, 1), :] = jnp.sum(piece, axis=0, keepdims=True)

    @pl.when(step == pl.num_programs(0) - 1)
    def _():
        for dest in range(out.shape[0]):
            out[dest] = sums[...]


def potential_kernel(tile_list, arrived, basis, out, scales, acc, *, n_row, n_col, comps, half_tile, width):
    step = pl.program_id(0)
    my_row = lax.axis_index("row")
    my_col = lax.axis_index("col")
    half = lax.axis_index("grid")
    span = comps * half_tile
    points = basis.shape[0] * basis.shape[2]
    n_half = basis.shape[0]
    half_points = basis.shape[2]

    @pl.when(step == 0)
    def _():
        acc[...] = jnp.zeros_like(acc)
        dens = jnp.sum(arrived[:, 0:comps], axis=0)
        total = dens[0]
        spin = [dens[comp] for comp in range(1, comps)]
        norm = jnp.sqrt(1.0 + sum(s * s for s in spin))
        potentials = [total / jnp.sqrt(1.0 + total * total)] + [s / norm for s in spin]
        weights = jnp.concatenate(
            [
                jnp.concatenate(
                    [arrived[q * n_half + h, comps, 0:1, 0:half_points] for h in range(n_half)], axis=1
                )
                for q in range(n_row)
            ],
            axis=0,
        )
        for comp in range(comps):
            scales[comp] = potentials[comp] * weights

    columns, slot, multiple, present = find(tile_list, step * n_col + my_col, n_row, my_row)

    @pl.when(present)
    def _():
        samples = basis[:, 0].reshape(points, basis.shape[3])
        rows = own_rows(basis, slot, half, width, half_tile)
        weighted = jnp.concatenate(
            [(rows * scales[comp, pl.ds(step, 1), :]).astype(jnp.bfloat16) for comp in range(comps)], axis=0
        )
        part = jnp.dot(weighted, samples, preferred_element_type=jnp.float32)
        first = pl.multiple_of(multiple * span, span)
        for s, tile in enumerate(columns):
            acc[tile, pl.ds(first, span), :] += part[:, s * width : (s + 1) * width]

    @pl.when(step == pl.num_programs(0) - 1)
    def _():
        out[...] = acc[...].astype(jnp.bfloat16)


def update_kernel(pieces, density, first, copies):
    total = jnp.sum(pieces[...].astype(jnp.float32), axis=0).astype(jnp.bfloat16)
    first[...] = total
    updated = (density[...].astype(jnp.float32) + MIXING * total.astype(jnp.float32)).astype(jnp.bfloat16)
    for dest in range(copies.shape[0]):
        copies[dest] = updated


def sum_kernel(pieces, out):
    out[...] = jnp.sum(pieces[...].astype(jnp.float32), axis=0).astype(jnp.bfloat16)


def body(density, basis_values, quad_weight, screen, tile_list):
    n_row = lax.axis_size("row")
    n_col = lax.axis_size("col")
    n_grid = lax.axis_size("grid")
    row_tiles, _, comps, half_tile, width = density.shape
    half_points, functions = basis_values.shape[1:]
    points = half_points * n_grid
    rows = row_tiles * comps * half_tile
    span = comps * half_tile
    planes = comps + 1
    sizes = dict(n_row=n_row, n_col=n_col, comps=comps, half_tile=half_tile, width=width)
    own = density.reshape(rows, width)
    basis = lax.all_gather(basis_values, "row", axis=0, tiled=True)
    basis = lax.all_gather(basis, "grid", axis=0, tiled=False)
    params = pltpu.CompilerParams(dimension_semantics=("arbitrary",), vmem_limit_bytes=VMEM_BYTES)
    basis_spec = pl.BlockSpec((n_grid, 1, half_points, functions), lambda b, t: (0, b, 0, 0))
    whole = lambda *shape: pl.BlockSpec(shape, lambda b, t: (0,) * len(shape))
    message = (n_row * n_grid, planes, n_row, points)
    densities = pl.pallas_call(
        functools.partial(density_kernel, **sizes),
        grid_spec=pltpu.PrefetchScalarGridSpec(
            num_scalar_prefetch=1,
            grid=(n_row,),
            in_specs=[whole(n_col, rows, width), basis_spec, whole(1, half_points), whole(1, half_points)],
            out_specs=whole(*message),
            scratch_shapes=[
                pltpu.VMEM((span, functions), jnp.bfloat16),
                pltpu.VMEM((planes, n_row, points), jnp.float32),
            ],
        ),
        out_shape=jax.ShapeDtypeStruct(message, jnp.float32),
        compiler_params=params,
    )
    potentials = pl.pallas_call(
        functools.partial(potential_kernel, **sizes),
        grid_spec=pltpu.PrefetchScalarGridSpec(
            num_scalar_prefetch=1,
            grid=(n_row,),
            in_specs=[whole(*message), basis_spec],
            out_specs=whole(n_col, rows, width),
            scratch_shapes=[
                pltpu.VMEM((comps, n_row, points), jnp.float32),
                pltpu.VMEM((n_col, rows, width), jnp.float32),
            ],
        ),
        out_shape=jax.ShapeDtypeStruct((n_col, rows, width), jnp.bfloat16),
        compiler_params=params,
    )
    chunk = rows // 4
    pieces_spec = pl.BlockSpec((n_col, chunk, width), lambda i: (0, i, 0))
    row_spec = pl.BlockSpec((chunk, width), lambda i: (i, 0))
    owned = jax.ShapeDtypeStruct((rows, width), jnp.bfloat16)
    update = pl.pallas_call(
        update_kernel,
        grid=(rows // chunk,),
        in_specs=[pieces_spec, row_spec],
        out_specs=[row_spec, pieces_spec],
        out_shape=[owned, jax.ShapeDtypeStruct((n_col, rows, width), jnp.bfloat16)],
        compiler_params=params,
    )
    add_up = pl.pallas_call(
        sum_kernel,
        grid=(rows // chunk,),
        in_specs=[pieces_spec],
        out_specs=row_spec,
        out_shape=owned,
        compiler_params=params,
    )

    def build(copies):
        strip = lax.all_to_all(copies, "col", 0, 0, tiled=True)
        partials = densities(tile_list, strip, basis, quad_weight, screen)
        arrived = lax.all_to_all(partials, ("row", "grid"), 0, 0, tiled=True)
        slabs = potentials(tile_list, arrived, basis)
        return lax.all_to_all(slabs, "col", 0, 0, tiled=True)

    first, copies = update(build(everyone(own, n_col)), own)
    second = add_up(build(copies))
    shape = density.shape
    return first.reshape(shape), second.reshape(shape)


def solution(mesh):
    in_specs = (
        P(None, "row", None, "grid", "col"),
        P(("row", "col"), "grid", None),
        P(("row", "col"), "grid"),
        P(("row", "col"), "grid"),
        P(),
    )
    out_specs = (P(None, "row", None, "grid", "col"), P(None, "row", None, "grid", "col"))
    return jax.shard_map(body, mesh=mesh, in_specs=in_specs, out_specs=out_specs, check_vma=False)
```

```python
import functools

import jax
import jax.numpy as jnp
from jax import lax
from jax.experimental import pallas as pl
from jax.experimental.pallas import tpu as pltpu
from jax.sharding import PartitionSpec as P

MIXING = 0.001
VMEM_BYTES = 32 * 1024 * 1024


def everyone(x, n):
    return jnp.broadcast_to(x[None], (n, *x.shape))


def find(tile_list, batch, n_row, my_row):
    columns = [tile_list[batch, s] for s in range(tile_list.shape[1])]
    slot = jnp.int32(0)
    multiple = jnp.int32(0)
    present = jnp.bool_(False)
    for s, tile in enumerate(columns):
        match = lax.rem(tile, n_row) == my_row
        slot = jnp.where(match, s, slot)
        multiple = jnp.where(match, lax.div(tile, n_row), multiple)
        present = jnp.logical_or(present, match)
    return columns, slot, multiple, present


def own_rows(basis, slot, half, tile_width, half_tile):
    points = basis.shape[1] * basis.shape[2]
    block = basis[0, :, :, pl.ds(pl.multiple_of(slot * tile_width, tile_width), tile_width)]
    block = block.reshape(points, tile_width)
    rows = lax.broadcasted_iota(jnp.int32, (half_tile, tile_width), 0) + half * half_tile
    lanes = lax.broadcasted_iota(jnp.int32, (half_tile, tile_width), 1)
    chosen = jnp.where(rows == lanes, 1.0, 0.0).astype(jnp.bfloat16)
    return lax.dot_general(chosen, block, (((1,), (1,)), ((), ())), preferred_element_type=jnp.float32)


def density_kernel(tile_list, strip, basis, weight, screen, out, block, sums, *, n_row, n_col, comps, half_tile, width):
    step = pl.program_id(0)
    my_row = lax.axis_index("row")
    my_col = lax.axis_index("col")
    half = lax.axis_index("grid")
    span = comps * half_tile
    n_half, half_points, functions = basis.shape[1:]

    @pl.when(step == 0)
    def _():
        sums[...] = jnp.zeros_like(sums)

    columns, slot, multiple, present = find(tile_list, step * n_col + my_col, n_row, my_row)

    @pl.when(present)
    def _():
        for s, tile in enumerate(columns):
            first = pl.multiple_of(multiple * span, span)
            block[:, s * width : (s + 1) * width] = strip[tile, pl.ds(first, span), :]
        samples = basis[0].reshape(n_half * half_points, functions)
        part = lax.dot_general(
            block[...], samples, (((1,), (1,)), ((), ())), preferred_element_type=jnp.float32
        )
        rows = own_rows(basis, slot, half, width, half_tile)
        for comp in range(comps):
            piece = part[comp * half_tile : (comp + 1) * half_tile, :] * rows
            sums[comp, pl.ds(step, 1), :] = jnp.sum(piece, axis=0, keepdims=True)

    @pl.when(step == pl.num_programs(0) - 1)
    def _():
        own = weight[...] * screen[...].astype(jnp.float32)
        for dest in range(out.shape[0]):
            h = dest % n_half
            out[dest, 0:comps] = sums[:, :, h * half_points : (h + 1) * half_points]
            if out.shape[1] > comps:
                out[dest, comps] = jnp.broadcast_to(own, out.shape[2:])


def scales_of(dens, weights):
    total = dens[0]
    spin = [dens[comp] for comp in range(1, dens.shape[0])]
    norm = jnp.sqrt(1.0 + sum(s * s for s in spin))
    potentials = [total / jnp.sqrt(1.0 + total * total)] + [s / norm for s in spin]
    return [potential * weights for potential in potentials]


def first_scale_kernel(arrived, scales, weights):
    comps = scales.shape[0]
    n_row = weights.shape[0]
    half = lax.axis_index("grid")
    n_half = arrived.shape[0] // n_row
    for q in range(n_row):
        weights[q : q + 1, :] = arrived[q * n_half + half, comps, 0:1, :]
    for comp, scale in enumerate(scales_of(jnp.sum(arrived[:, 0:comps], axis=0), weights[...])):
        scales[comp] = scale


def scale_kernel(arrived, weights, scales):
    for comp, scale in enumerate(scales_of(jnp.sum(arrived[...], axis=0), weights[...])):
        scales[comp] = scale


def potential_kernel(tile_list, own, other, basis, out, scales, acc, *, n_row, n_col, comps, half_tile, width):
    step = pl.program_id(0)
    my_row = lax.axis_index("row")
    my_col = lax.axis_index("col")
    half = lax.axis_index("grid")
    span = comps * half_tile
    n_half, half_points, functions = basis.shape[1:]

    @pl.when(step == 0)
    def _():
        acc[...] = jnp.zeros_like(acc)
        scales[:, :, pl.ds(pl.multiple_of(half * half_points, half_points), half_points)] = own[...]
        scales[:, :, pl.ds(pl.multiple_of((1 - half) * half_points, half_points), half_points)] = other[...]

    columns, slot, multiple, present = find(tile_list, step * n_col + my_col, n_row, my_row)

    @pl.when(present)
    def _():
        samples = basis[0].reshape(n_half * half_points, functions)
        rows = own_rows(basis, slot, half, width, half_tile)
        weighted = jnp.concatenate(
            [(rows * scales[comp, pl.ds(step, 1), :]).astype(jnp.bfloat16) for comp in range(comps)], axis=0
        )
        part = jnp.dot(weighted, samples, preferred_element_type=jnp.float32)
        first = pl.multiple_of(multiple * span, span)
        for s, tile in enumerate(columns):
            acc[tile, pl.ds(first, span), :] += part[:, s * width : (s + 1) * width]

    @pl.when(step == pl.num_programs(0) - 1)
    def _():
        out[...] = acc[...].astype(jnp.bfloat16)


def update_kernel(pieces, density, first, copies):
    total = jnp.sum(pieces[...].astype(jnp.float32), axis=0).astype(jnp.bfloat16)
    first[...] = total
    updated = (density[...].astype(jnp.float32) + MIXING * total.astype(jnp.float32)).astype(jnp.bfloat16)
    for dest in range(copies.shape[0]):
        copies[dest] = updated


def sum_kernel(pieces, out):
    out[...] = jnp.sum(pieces[...].astype(jnp.float32), axis=0).astype(jnp.bfloat16)


def body(density, basis_values, quad_weight, screen, tile_list):
    n_row = lax.axis_size("row")
    n_col = lax.axis_size("col")
    n_grid = lax.axis_size("grid")
    row_tiles, _, comps, half_tile, width = density.shape
    half_points, functions = basis_values.shape[1:]
    points = half_points * n_grid
    rows = row_tiles * comps * half_tile
    span = comps * half_tile
    sizes = dict(n_row=n_row, n_col=n_col, comps=comps, half_tile=half_tile, width=width)
    own = density.reshape(rows, width)
    basis = lax.all_gather(basis_values, ("row", "grid"), axis=0, tiled=True)
    basis = basis.reshape(n_row, n_grid, half_points, functions)
    params = pltpu.CompilerParams(dimension_semantics=("arbitrary",), vmem_limit_bytes=VMEM_BYTES)
    basis_spec = pl.BlockSpec((1, n_grid, half_points, functions), lambda b, t: (b, 0, 0, 0))
    whole = lambda *shape: pl.BlockSpec(shape, lambda b, t: (0,) * len(shape))
    scale = jax.ShapeDtypeStruct((comps, n_row, half_points), jnp.float32)
    kept = jax.ShapeDtypeStruct((n_row, half_points), jnp.float32)

    def densities(planes):
        message = (n_row * n_grid, planes, n_row, half_points)
        return pl.pallas_call(
            functools.partial(density_kernel, **sizes),
            grid_spec=pltpu.PrefetchScalarGridSpec(
                num_scalar_prefetch=1,
                grid=(n_row,),
                in_specs=[whole(n_col, rows, width), basis_spec, whole(1, half_points), whole(1, half_points)],
                out_specs=whole(*message),
                scratch_shapes=[
                    pltpu.VMEM((span, functions), jnp.bfloat16),
                    pltpu.VMEM((comps, n_row, points), jnp.float32),
                ],
            ),
            out_shape=jax.ShapeDtypeStruct(message, jnp.float32),
            compiler_params=params,
        )

    first_scales = pl.pallas_call(first_scale_kernel, out_shape=[scale, kept])
    scales = pl.pallas_call(scale_kernel, out_shape=scale)
    potentials = pl.pallas_call(
        functools.partial(potential_kernel, **sizes),
        grid_spec=pltpu.PrefetchScalarGridSpec(
            num_scalar_prefetch=1,
            grid=(n_row,),
            in_specs=[whole(*scale.shape), whole(*scale.shape), basis_spec],
            out_specs=whole(n_col, rows, width),
            scratch_shapes=[
                pltpu.VMEM((comps, n_row, points), jnp.float32),
                pltpu.VMEM((n_col, rows, width), jnp.float32),
            ],
        ),
        out_shape=jax.ShapeDtypeStruct((n_col, rows, width), jnp.bfloat16),
        compiler_params=params,
    )
    chunk = rows // 4
    pieces_spec = pl.BlockSpec((n_col, chunk, width), lambda i: (0, i, 0))
    row_spec = pl.BlockSpec((chunk, width), lambda i: (i, 0))
    owned = jax.ShapeDtypeStruct((rows, width), jnp.bfloat16)
    update = pl.pallas_call(
        update_kernel,
        grid=(rows // chunk,),
        in_specs=[pieces_spec, row_spec],
        out_specs=[row_spec, pieces_spec],
        out_shape=[owned, jax.ShapeDtypeStruct((n_col, rows, width), jnp.bfloat16)],
        compiler_params=params,
    )
    add_up = pl.pallas_call(
        sum_kernel,
        grid=(rows // chunk,),
        in_specs=[pieces_spec],
        out_specs=row_spec,
        out_shape=owned,
        compiler_params=params,
    )

    def partials(copies, planes):
        strip = lax.all_to_all(copies, "col", 0, 0, tiled=True)
        partial = densities(planes)(tile_list, strip, basis, quad_weight, screen)
        return lax.all_to_all(partial, ("row", "grid"), 0, 0, tiled=True)

    def slabs(mine):
        other = lax.ppermute(mine, "grid", [(0, 1), (1, 0)])
        return lax.all_to_all(potentials(tile_list, mine, other, basis), "col", 0, 0, tiled=True)

    mine, weights = first_scales(partials(everyone(own, n_col), comps + 1))
    first, copies = update(slabs(mine), own)
    second = add_up(slabs(scales(partials(copies, comps), weights)))
    shape = density.shape
    return first.reshape(shape), second.reshape(shape)


def solution(mesh):
    in_specs = (
        P(None, "row", None, "grid", "col"),
        P(("row", "col"), "grid", None),
        P(("row", "col"), "grid"),
        P(("row", "col"), "grid"),
        P(),
    )
    out_specs = (P(None, "row", None, "grid", "col"), P(None, "row", None, "grid", "col"))
    return jax.shard_map(body, mesh=mesh, in_specs=in_specs, out_specs=out_specs, check_vma=False)
```

```python
import functools

import jax
import jax.numpy as jnp
from jax import lax
from jax.experimental import pallas as pl
from jax.experimental.pallas import tpu as pltpu
from jax.sharding import PartitionSpec as P

MIXING = 0.001
VMEM_BYTES = 32 * 1024 * 1024


def everyone(x, n):
    return jnp.broadcast_to(x[None], (n, *x.shape))


def find(tile_list, batch, n_row, my_row):
    columns = [tile_list[batch, s] for s in range(tile_list.shape[1])]
    slot = jnp.int32(0)
    multiple = jnp.int32(0)
    present = jnp.bool_(False)
    for s, tile in enumerate(columns):
        match = lax.rem(tile, n_row) == my_row
        slot = jnp.where(match, s, slot)
        multiple = jnp.where(match, lax.div(tile, n_row), multiple)
        present = jnp.logical_or(present, match)
    return columns, slot, multiple, present


def own_rows(basis, batch, slot, half, tile_width, half_tile):
    points = basis.shape[1] * basis.shape[2]
    block = basis[batch, :, :, pl.ds(pl.multiple_of(slot * tile_width, tile_width), tile_width)]
    block = block.reshape(points, tile_width)
    rows = lax.broadcasted_iota(jnp.int32, (half_tile, tile_width), 0) + half * half_tile
    lanes = lax.broadcasted_iota(jnp.int32, (half_tile, tile_width), 1)
    chosen = jnp.where(rows == lanes, 1.0, 0.0).astype(jnp.bfloat16)
    return lax.dot_general(chosen, block, (((1,), (1,)), ((), ())), preferred_element_type=jnp.float32)


def add_densities(tile_list, strip, basis, arrival, weight, screen, out, sums, *, n_col, comps, half_tile, width):
    my_row = lax.axis_index("row")
    my_col = lax.axis_index("col")
    half = lax.axis_index("grid")
    span = comps * half_tile
    n_row, n_half, half_points, functions = basis.shape
    for batch in range(n_row):
        arrival(batch)
        columns, slot, multiple, present = find(tile_list, batch * n_col + my_col, n_row, my_row)
        first = pl.multiple_of(multiple * span, span)
        block = jnp.concatenate([strip[tile, pl.ds(first, span), :] for tile in columns], axis=1)
        samples = basis[batch].reshape(n_half * half_points, functions)
        part = lax.dot_general(block, samples, (((1,), (1,)), ((), ())), preferred_element_type=jnp.float32)
        rows = own_rows(basis, batch, slot, half, width, half_tile)
        for comp in range(comps):
            piece = part[comp * half_tile : (comp + 1) * half_tile, :] * rows
            total = jnp.sum(piece, axis=0, keepdims=True)
            sums[comp, batch : batch + 1, :] = jnp.where(present, total, 0.0)
    own = weight[...] * screen[...].astype(jnp.float32)
    for dest in range(out.shape[0]):
        h = dest % n_half
        out[dest, 0:comps] = sums[:, :, h * half_points : (h + 1) * half_points]
        if out.shape[1] > comps:
            out[dest, comps] = jnp.broadcast_to(own, out.shape[2:])


def first_density_kernel(tile_list, strip_far, basis_far, weight, screen, out, strip, basis, sums, sems, **sizes):
    n_row = basis.shape[0]
    strip_copy = pltpu.make_async_copy(strip_far, strip, sems.at[n_row])
    basis_copies = [
        pltpu.make_async_copy(basis_far.at[batch], basis.at[batch], sems.at[batch]) for batch in range(n_row)
    ]
    strip_copy.start()
    for copy in basis_copies:
        copy.start()
    strip_copy.wait()
    arrival = lambda batch: basis_copies[batch].wait()
    add_densities(tile_list, strip, basis, arrival, weight, screen, out, sums, **sizes)


def density_kernel(tile_list, strip, basis, weight, screen, out, sums, **sizes):
    add_densities(tile_list, strip, basis, lambda batch: None, weight, screen, out, sums, **sizes)


def scales_of(dens, weights):
    total = dens[0]
    spin = [dens[comp] for comp in range(1, dens.shape[0])]
    norm = jnp.sqrt(1.0 + sum(s * s for s in spin))
    potentials = [total / jnp.sqrt(1.0 + total * total)] + [s / norm for s in spin]
    return [potential * weights for potential in potentials]


def first_scale_kernel(arrived, scales, weights):
    comps = scales.shape[0]
    n_row = weights.shape[0]
    half = lax.axis_index("grid")
    n_half = arrived.shape[0] // n_row
    for q in range(n_row):
        weights[q : q + 1, :] = arrived[q * n_half + half, comps, 0:1, :]
    for comp, scale in enumerate(scales_of(jnp.sum(arrived[:, 0:comps], axis=0), weights[...])):
        scales[comp] = scale


def scale_kernel(arrived, weights, scales):
    for comp, scale in enumerate(scales_of(jnp.sum(arrived[...], axis=0), weights[...])):
        scales[comp] = scale


def potential_kernel(tile_list, own, other, basis, out, scales, acc, seen, *, n_col, comps, half_tile, width):
    my_row = lax.axis_index("row")
    my_col = lax.axis_index("col")
    half = lax.axis_index("grid")
    span = comps * half_tile
    n_row, n_half, half_points, functions = basis.shape
    for tile in range(acc.shape[0]):
        for multiple in range(acc.shape[1] // span):
            seen[tile, multiple] = 0
    scales[:, :, pl.ds(pl.multiple_of(half * half_points, half_points), half_points)] = own[...]
    scales[:, :, pl.ds(pl.multiple_of((1 - half) * half_points, half_points), half_points)] = other[...]

    for batch in range(n_row):
        columns, slot, multiple, present = find(tile_list, batch * n_col + my_col, n_row, my_row)
        samples = basis[batch].reshape(n_half * half_points, functions)
        rows = own_rows(basis, batch, slot, half, width, half_tile)
        rows = jnp.where(present, rows, 0.0)
        weighted = jnp.concatenate(
            [(rows * scales[comp, batch : batch + 1, :]).astype(jnp.bfloat16) for comp in range(comps)], axis=0
        )
        part = jnp.dot(weighted, samples, preferred_element_type=jnp.float32)
        first = pl.multiple_of(multiple * span, span)
        for s, tile in enumerate(columns):
            before = jnp.where(seen[tile, multiple] > 0, acc[tile, pl.ds(first, span), :], 0.0)
            acc[tile, pl.ds(first, span), :] = before + part[:, s * width : (s + 1) * width]
            seen[tile, multiple] = 1
    for tile in range(acc.shape[0]):
        for multiple in range(acc.shape[1] // span):
            rows = slice(multiple * span, (multiple + 1) * span)
            out[tile, rows, :] = jnp.where(seen[tile, multiple] > 0, acc[tile, rows, :], 0.0).astype(jnp.bfloat16)


def update_kernel(pieces, density, first, copies):
    total = jnp.sum(pieces[...].astype(jnp.float32), axis=0).astype(jnp.bfloat16)
    first[...] = total
    updated = (density[...].astype(jnp.float32) + MIXING * total.astype(jnp.float32)).astype(jnp.bfloat16)
    for dest in range(copies.shape[0]):
        copies[dest] = updated


def sum_kernel(pieces, out):
    out[...] = jnp.sum(pieces[...].astype(jnp.float32), axis=0).astype(jnp.bfloat16)


def body(density, basis_values, quad_weight, screen, tile_list):
    n_row = lax.axis_size("row")
    n_col = lax.axis_size("col")
    n_grid = lax.axis_size("grid")
    row_tiles, _, comps, half_tile, width = density.shape
    half_points, functions = basis_values.shape[1:]
    points = half_points * n_grid
    rows = row_tiles * comps * half_tile
    span = comps * half_tile
    sizes = dict(n_col=n_col, comps=comps, half_tile=half_tile, width=width)
    own = density.reshape(rows, width)
    basis = lax.all_gather(basis_values, ("row", "grid"), axis=0, tiled=True)
    basis = basis.reshape(n_row, n_grid, half_points, functions)
    params = pltpu.CompilerParams(vmem_limit_bytes=VMEM_BYTES)
    in_smem = pl.BlockSpec(memory_space=pltpu.SMEM)
    in_vmem = pl.BlockSpec(memory_space=pltpu.VMEM)
    scale = jax.ShapeDtypeStruct((comps, n_row, half_points), jnp.float32)
    kept = jax.ShapeDtypeStruct((n_row, half_points), jnp.float32)

    in_hbm = pl.BlockSpec(memory_space=pltpu.HBM)
    sums = pltpu.VMEM((comps, n_row, points), jnp.float32)
    message = lambda planes: jax.ShapeDtypeStruct((n_row * n_grid, planes, n_row, half_points), jnp.float32)
    first_densities = pl.pallas_call(
        functools.partial(first_density_kernel, **sizes),
        in_specs=[in_smem, in_hbm, in_hbm, in_vmem, in_vmem],
        out_specs=in_vmem,
        scratch_shapes=[
            pltpu.VMEM((n_col, rows, width), jnp.bfloat16),
            pltpu.VMEM((n_row, n_grid, half_points, functions), jnp.bfloat16),
            sums,
            pltpu.SemaphoreType.DMA((n_row + 1,)),
        ],
        out_shape=message(comps + 1),
        compiler_params=params,
    )
    densities = pl.pallas_call(
        functools.partial(density_kernel, **sizes),
        in_specs=[in_smem, in_vmem, in_vmem, in_vmem, in_vmem],
        out_specs=in_vmem,
        scratch_shapes=[sums],
        out_shape=message(comps),
        compiler_params=params,
    )
    first_scales = pl.pallas_call(
        first_scale_kernel, in_specs=[in_vmem], out_specs=[in_vmem, in_vmem], out_shape=[scale, kept]
    )
    scales = pl.pallas_call(scale_kernel, in_specs=[in_vmem, in_vmem], out_specs=in_vmem, out_shape=scale)
    potentials = pl.pallas_call(
        functools.partial(potential_kernel, **sizes),
        in_specs=[in_smem, in_vmem, in_vmem, in_vmem],
        out_specs=in_vmem,
        scratch_shapes=[
            pltpu.VMEM((comps, n_row, points), jnp.float32),
            pltpu.VMEM((n_col, rows, width), jnp.float32),
            pltpu.SMEM((n_col, row_tiles), jnp.int32),
        ],
        out_shape=jax.ShapeDtypeStruct((n_col, rows, width), jnp.bfloat16),
        compiler_params=params,
    )
    owned = jax.ShapeDtypeStruct((rows, width), jnp.bfloat16)
    update = pl.pallas_call(
        update_kernel,
        in_specs=[in_vmem, in_vmem],
        out_specs=[in_vmem, in_vmem],
        out_shape=[owned, jax.ShapeDtypeStruct((n_col, rows, width), jnp.bfloat16)],
        compiler_params=params,
    )
    add_up = pl.pallas_call(
        sum_kernel, in_specs=[in_vmem], out_specs=in_vmem, out_shape=owned, compiler_params=params
    )

    def partials(kernel, copies, space):
        strip = lax.all_to_all(copies, "col", 0, 0, tiled=True)
        operands = [pltpu.with_memory_space_constraint(x, space) for x in (strip, basis)]
        partial = kernel(tile_list, *operands, quad_weight, screen)
        arrived = lax.all_to_all(partial, ("row", "grid"), 0, 0, tiled=True)
        return pltpu.with_memory_space_constraint(arrived, pltpu.VMEM)

    def slabs(mine):
        other = lax.ppermute(mine, "grid", [(0, 1), (1, 0)])
        return lax.all_to_all(potentials(tile_list, mine, other, basis), "col", 0, 0, tiled=True)

    mine, weights = first_scales(partials(first_densities, everyone(own, n_col), pltpu.HBM))
    first, copies = update(slabs(mine), own)
    second = add_up(slabs(scales(partials(densities, copies, pltpu.VMEM), weights)))
    shape = density.shape
    return first.reshape(shape), second.reshape(shape)


def solution(mesh):
    in_specs = (
        P(None, "row", None, "grid", "col"),
        P(("row", "col"), "grid", None),
        P(("row", "col"), "grid"),
        P(("row", "col"), "grid"),
        P(),
    )
    out_specs = (P(None, "row", None, "grid", "col"), P(None, "row", None, "grid", "col"))
    return jax.shard_map(body, mesh=mesh, in_specs=in_specs, out_specs=out_specs, check_vma=False)
```

```python
import functools

import jax
import jax.numpy as jnp
from jax import lax
from jax.experimental import pallas as pl
from jax.experimental.pallas import tpu as pltpu
from jax.sharding import PartitionSpec as P

MIXING = 0.001
VMEM_BYTES = 32 * 1024 * 1024


def everyone(x, n):
    return jnp.broadcast_to(x[None], (n, *x.shape))


def owned_multiple(row, tile, n_row, where=jnp.where, div=lax.div, rem=lax.rem):
    high = div(tile, n_row)
    return where(row <= rem(tile, n_row), high, 1 - high)


def partner(row, col, n_row):
    plain = dict(where=lambda a, b, c: b if a else c, div=lambda a, b: a // b, rem=lambda a, b: a % b)
    return col % n_row, owned_multiple(row, col, n_row, **plain) * n_row + row


def exchanges(n_row, n_col, n_grid, back):
    pairs = []
    for row in range(n_row):
        for col in range(n_col):
            to_row, to_col = partner(row, col, n_row)
            for core in range(n_grid):
                here = (row * n_col + col) * n_grid + core
                there = (to_row * n_col + to_col) * n_grid + core
                pairs.append((there, here) if back else (here, there))
    return pairs


def swapped(x):
    n = x.shape[1]
    rows = lax.broadcasted_iota(jnp.int32, (n, n), 0)
    lanes = lax.broadcasted_iota(jnp.int32, (n, n), 1)
    unit = jnp.where(rows == lanes, 1.0, 0.0).astype(jnp.bfloat16)
    return lax.dot_general(unit, x, (((1,), (1,)), ((), ())), preferred_element_type=jnp.float32)


def turn(tile, turned):
    width = tile.shape[1]
    for pair in range(turned.shape[0]):
        turned[pair] = swapped(tile[pair * width : (pair + 1) * width, :]).astype(jnp.bfloat16)


def joined(own, other, half):
    pairs, width = own.shape[:2]
    rows = pl.ds(pl.multiple_of(half * (width // 2), width // 2), width // 2)
    left = lax.broadcasted_iota(jnp.int32, (width // 2, width), 1) < width // 2
    comps = []
    for pair in range(pairs):
        mine = own[pair, rows, :].astype(jnp.float32)
        theirs = other[pair, rows, :].astype(jnp.float32)
        low = jnp.where(half == 0, mine, theirs)
        high = jnp.where(half == 0, theirs, mine)
        comps.append(jnp.where(left, low, pltpu.roll(high, width // 2, 1)))
        comps.append(jnp.where(left, pltpu.roll(low, width // 2, 1), high))
    return jnp.concatenate(comps, axis=0)


def find(tile_list, batch, n_row, my_row):
    columns = [tile_list[batch, s] for s in range(tile_list.shape[1])]
    slot = jnp.int32(0)
    multiple = jnp.int32(0)
    present = jnp.bool_(False)
    for s, tile in enumerate(columns):
        match = lax.rem(tile, n_row) == my_row
        slot = jnp.where(match, s, slot)
        multiple = jnp.where(match, lax.div(tile, n_row), multiple)
        present = jnp.logical_or(present, match)
    owned = [jnp.logical_and(present, owned_multiple(my_row, tile, n_row) == multiple) for tile in columns]
    return columns, slot, multiple, present, owned


def own_rows(basis, batch, slot, half, tile_width, half_tile):
    points = basis.shape[1] * basis.shape[2]
    block = basis[batch, :, :, pl.ds(pl.multiple_of(slot * tile_width, tile_width), tile_width)]
    block = block.reshape(points, tile_width)
    rows = lax.broadcasted_iota(jnp.int32, (half_tile, tile_width), 0) + half * half_tile
    lanes = lax.broadcasted_iota(jnp.int32, (half_tile, tile_width), 1)
    chosen = jnp.where(rows == lanes, 1.0, 0.0).astype(jnp.bfloat16)
    return lax.dot_general(chosen, block, (((1,), (1,)), ((), ())), preferred_element_type=jnp.float32)


def turn_kernel(density, turned, *, n_row, span):
    my_row = lax.axis_index("row")
    my_col = lax.axis_index("col")
    other = 1 - owned_multiple(my_row, my_col, n_row)
    turn(density[pl.ds(pl.multiple_of(other * span, span), span), :], turned)


def symmetric_kernel(density, mine, theirs, total, copies, *, n_row, span):
    my_row = lax.axis_index("row")
    my_col = lax.axis_index("col")
    half = lax.axis_index("grid")
    own = owned_multiple(my_row, my_col, n_row)
    tile = density[pl.ds(pl.multiple_of(own * span, span), span), :].astype(jnp.float32)
    mirror = joined(mine, theirs, half)
    tile = tile + jnp.where(lax.rem(my_col, n_row) == my_row, 0.0, mirror)
    total[...] = tile
    rounded = tile.astype(jnp.bfloat16)
    for dest in range(copies.shape[0]):
        copies[dest] = rounded


def add_densities(tile_list, strip, basis, arrival, weight, screen, out, sums, *, n_col, comps, half_tile, width):
    my_row = lax.axis_index("row")
    my_col = lax.axis_index("col")
    half = lax.axis_index("grid")
    n_row, n_half, half_points, functions = basis.shape
    nothing = jnp.zeros(strip.shape[1:], strip.dtype)
    for batch in range(n_row):
        columns, slot, multiple, present, owned = find(tile_list, batch * n_col + my_col, n_row, my_row)
        block = jnp.concatenate(
            [jnp.where(mine, strip[tile], nothing) for tile, mine in zip(columns, owned)], axis=1
        )
        arrival(batch)
        samples = basis[batch].reshape(n_half * half_points, functions)
        part = lax.dot_general(block, samples, (((1,), (1,)), ((), ())), preferred_element_type=jnp.float32)
        rows = own_rows(basis, batch, slot, half, width, half_tile)
        for comp in range(comps):
            piece = part[comp * half_tile : (comp + 1) * half_tile, :] * rows
            sums[comp, batch : batch + 1, :] = jnp.sum(piece, axis=0, keepdims=True)
    own = weight[...] * screen[...].astype(jnp.float32)
    for dest in range(out.shape[0]):
        h = dest % n_half
        out[dest, 0:comps] = sums[:, :, h * half_points : (h + 1) * half_points]
        if out.shape[1] > comps:
            out[dest, comps] = jnp.broadcast_to(own, out.shape[2:])


def first_density_kernel(tile_list, strip, basis_far, weight, screen, out, basis, sums, sems, **sizes):
    groups = sems.shape[0]
    size = basis.shape[0] // groups
    copies = [
        pltpu.make_async_copy(basis_far.at[pl.ds(g * size, size)], basis.at[pl.ds(g * size, size)], sems.at[g])
        for g in range(groups)
    ]
    for copy in copies:
        copy.start()

    def arrival(batch):
        if batch % size == 0:
            copies[batch // size].wait()

    add_densities(tile_list, strip, basis, arrival, weight, screen, out, sums, **sizes)


def density_kernel(tile_list, strip, basis, weight, screen, out, sums, **sizes):
    add_densities(tile_list, strip, basis, lambda batch: None, weight, screen, out, sums, **sizes)


def scales_of(dens, weights):
    total = dens[0]
    spin = [dens[comp] for comp in range(1, dens.shape[0])]
    norm = jnp.sqrt(1.0 + sum(s * s for s in spin))
    potentials = [total / jnp.sqrt(1.0 + total * total)] + [s / norm for s in spin]
    return [potential * weights for potential in potentials]


def first_scale_kernel(arrived, scales, weights):
    comps = scales.shape[0]
    n_row = weights.shape[0]
    half = lax.axis_index("grid")
    n_half = arrived.shape[0] // n_row
    for q in range(n_row):
        weights[q : q + 1, :] = arrived[q * n_half + half, comps, 0:1, :]
    for comp, scale in enumerate(scales_of(jnp.sum(arrived[:, 0:comps], axis=0), weights[...])):
        scales[comp] = scale


def scale_kernel(arrived, weights, scales):
    for comp, scale in enumerate(scales_of(jnp.sum(arrived[...], axis=0), weights[...])):
        scales[comp] = scale


def potential_kernel(tile_list, own, other, basis, out, scales, acc, seen, *, n_col, comps, half_tile, width):
    my_row = lax.axis_index("row")
    my_col = lax.axis_index("col")
    half = lax.axis_index("grid")
    n_row, n_half, half_points, functions = basis.shape
    multiples = out.shape[1]
    for tile in range(acc.shape[0]):
        for m in range(multiples):
            seen[tile, m] = 0
    scales[:, :, pl.ds(pl.multiple_of(half * half_points, half_points), half_points)] = own[...]
    scales[:, :, pl.ds(pl.multiple_of((1 - half) * half_points, half_points), half_points)] = other[...]
    for batch in range(n_row):
        columns, slot, multiple, present, owned = find(tile_list, batch * n_col + my_col, n_row, my_row)
        samples = basis[batch].reshape(n_half * half_points, functions)
        rows = own_rows(basis, batch, slot, half, width, half_tile)
        weighted = jnp.concatenate(
            [(rows * scales[comp, batch : batch + 1, :]).astype(jnp.bfloat16) for comp in range(comps)], axis=0
        )
        part = jnp.dot(weighted, samples, preferred_element_type=jnp.float32)
        m = 0 if multiples == 1 else multiple
        for s, tile in enumerate(columns):
            mine = owned[s] if multiples == 1 else present
            before = jnp.where(seen[tile, m] > 0, acc[tile, m], 0.0)
            acc[tile, m] = before + jnp.where(mine, part[:, s * width : (s + 1) * width], 0.0)
            seen[tile, m] = 1
    for tile in range(acc.shape[0]):
        for m in range(multiples):
            out[tile, m] = jnp.where(seen[tile, m] > 0, acc[tile, m], 0.0).astype(jnp.bfloat16)


def update_kernel(pieces, density, first, turned, copies, *, n_row):
    my_row = lax.axis_index("row")
    my_col = lax.axis_index("col")
    total = jnp.sum(pieces[...].astype(jnp.float32), axis=(0, 1)).astype(jnp.bfloat16)
    first[...] = total
    mixing = jnp.where(lax.rem(my_col, n_row) == my_row, MIXING, 2.0 * MIXING)
    updated = (density[...] + mixing * total.astype(jnp.float32)).astype(jnp.bfloat16)
    for dest in range(copies.shape[0]):
        copies[dest] = updated
    turn(total, turned)


def finish_kernel(pieces, first, mine, theirs, first_out, second_out, *, n_row):
    my_row = lax.axis_index("row")
    my_col = lax.axis_index("col")
    half = lax.axis_index("grid")
    own = owned_multiple(my_row, my_col, n_row)
    unpaired = lax.rem(my_col, n_row) == my_row
    second_out[...] = jnp.sum(pieces[...].astype(jnp.float32), axis=0).astype(jnp.bfloat16)
    first_out[own] = first[...]
    first_out[1 - own] = jnp.where(unpaired, 0.0, joined(mine, theirs, half)).astype(jnp.bfloat16)


def body(density, basis_values, quad_weight, screen, tile_list):
    n_row = lax.axis_size("row")
    n_col = lax.axis_size("col")
    n_grid = lax.axis_size("grid")
    row_tiles, _, comps, half_tile, width = density.shape
    half_points, functions = basis_values.shape[1:]
    points = half_points * n_grid
    rows = row_tiles * comps * half_tile
    span = comps * half_tile
    sizes = dict(n_col=n_col, comps=comps, half_tile=half_tile, width=width)
    own = density.reshape(rows, width)
    everywhere = ("row", "col", "grid")
    bf16 = lambda *shape: jax.ShapeDtypeStruct(shape, jnp.bfloat16)
    f32 = lambda *shape: jax.ShapeDtypeStruct(shape, jnp.float32)
    params = pltpu.CompilerParams(vmem_limit_bytes=VMEM_BYTES)
    smem = pl.BlockSpec(memory_space=pltpu.SMEM)
    hbm = pl.BlockSpec(memory_space=pltpu.HBM)
    vmem = pl.BlockSpec(memory_space=pltpu.VMEM)
    near = lambda x: pltpu.with_memory_space_constraint(x, pltpu.VMEM)

    def call(kernel, ins, outs, scratch=(), **settings):
        return pl.pallas_call(
            functools.partial(kernel, **settings),
            in_specs=ins,
            out_specs=[vmem] * len(outs),
            out_shape=outs,
            scratch_shapes=list(scratch),
            compiler_params=params,
        )

    block = (comps // n_grid, width, width)
    swap = [(0, 1), (1, 0)]
    sums = pltpu.VMEM((comps, n_row, points), jnp.float32)
    basis_shape = (n_row, n_grid, half_points, functions)
    basis_far = lax.all_gather(basis_values, ("row", "grid"), axis=0, tiled=True).reshape(basis_shape)

    def exchange(turned, back):
        mine = lax.ppermute(turned, everywhere, exchanges(n_row, n_col, n_grid, back))
        return mine, lax.ppermute(mine, "grid", swap)

    [turned] = call(turn_kernel, [vmem], [bf16(*block)], n_row=n_row, span=span)(own)
    symmetric, copies = call(
        symmetric_kernel, [vmem] * 3, [f32(span, width), bf16(n_col, span, width)], n_row=n_row, span=span
    )(own, *exchange(turned, True))

    def summed(partial):
        return near(lax.all_to_all(partial, ("row", "grid"), 0, 0, tiled=True))

    def slabs(mine, basis, multiples):
        other = lax.ppermute(mine, "grid", swap)
        shape = (n_col, multiples, span, width)
        [slab] = call(
            potential_kernel,
            [smem, vmem, vmem, vmem],
            [bf16(*shape)],
            [sums, pltpu.VMEM(shape, jnp.float32), pltpu.SMEM(shape[:2], jnp.int32)],
            **sizes,
        )(tile_list, near(mine), other, basis)
        return lax.all_to_all(slab, "col", 0, 0, tiled=True)

    message = (n_row * n_grid, comps, n_row, half_points)
    strip = near(lax.all_to_all(copies, "col", 0, 0, tiled=True))
    partial, basis = call(
        first_density_kernel,
        [smem, vmem, hbm, vmem, vmem],
        [f32(message[0], comps + 1, *message[2:]), bf16(*basis_shape)],
        [sums, pltpu.SemaphoreType.DMA((2,))],
        **sizes,
    )(tile_list, strip, pltpu.with_memory_space_constraint(basis_far, pltpu.HBM), quad_weight, screen)
    basis = near(basis)
    mine, weights = call(first_scale_kernel, [vmem], [f32(*message[1:]), f32(*message[2:])])(summed(partial))
    first, turned, copies = call(
        update_kernel, [vmem] * 2, [bf16(span, width), bf16(*block), bf16(n_col, span, width)], n_row=n_row
    )(slabs(mine, basis, 1), symmetric)
    mirrors = exchange(turned, False)
    strip = near(lax.all_to_all(copies, "col", 0, 0, tiled=True))
    [partial] = call(density_kernel, [smem] + [vmem] * 4, [f32(*message)], [sums], **sizes)(
        tile_list, strip, basis, quad_weight, screen
    )
    [mine] = call(scale_kernel, [vmem] * 2, [f32(*message[1:])])(summed(partial), near(weights))
    outs = call(finish_kernel, [vmem] * 4, [bf16(row_tiles, span, width)] * 2, n_row=n_row)(
        slabs(mine, basis, row_tiles), first, *mirrors
    )
    return tuple(out.reshape(density.shape) for out in outs)


def solution(mesh):
    in_specs = (
        P(None, "row", None, "grid", "col"),
        P(("row", "col"), "grid", None),
        P(("row", "col"), "grid"),
        P(("row", "col"), "grid"),
        P(),
    )
    out_specs = (P(None, "row", None, "grid", "col"), P(None, "row", None, "grid", "col"))
    return jax.shard_map(body, mesh=mesh, in_specs=in_specs, out_specs=out_specs, check_vma=False)
```

```python
import functools

import jax
import jax.numpy as jnp
from jax import lax
from jax.experimental import pallas as pl
from jax.experimental.pallas import tpu as pltpu
from jax.sharding import PartitionSpec as P

MIXING = 0.001
VMEM_BYTES = 32 * 1024 * 1024


def everyone(x, n):
    return jnp.broadcast_to(x[None], (n, *x.shape))


def owned_multiple(row, tile, n_row, where=jnp.where, div=lax.div, rem=lax.rem):
    high = div(tile, n_row)
    return where(row <= rem(tile, n_row), high, 1 - high)


def partner(row, col, n_row):
    plain = dict(where=lambda a, b, c: b if a else c, div=lambda a, b: a // b, rem=lambda a, b: a % b)
    return col % n_row, owned_multiple(row, col, n_row, **plain) * n_row + row


def exchanges(n_row, n_col, n_grid, back):
    pairs = []
    for row in range(n_row):
        for col in range(n_col):
            to_row, to_col = partner(row, col, n_row)
            for core in range(n_grid):
                here = (row * n_col + col) * n_grid + core
                there = (to_row * n_col + to_col) * n_grid + core
                pairs.append((there, here) if back else (here, there))
    return pairs


def swapped(x):
    n = x.shape[1]
    rows = lax.broadcasted_iota(jnp.int32, (n, n), 0)
    lanes = lax.broadcasted_iota(jnp.int32, (n, n), 1)
    unit = jnp.where(rows == lanes, 1.0, 0.0).astype(jnp.bfloat16)
    return lax.dot_general(unit, x, (((1,), (1,)), ((), ())), preferred_element_type=jnp.float32)


def turn(tile, turned):
    width = tile.shape[1]
    for pair in range(turned.shape[0]):
        turned[pair] = swapped(tile[pair * width : (pair + 1) * width, :]).astype(jnp.bfloat16)


def joined(own, other, half):
    pairs, width = own.shape[:2]
    rows = pl.ds(pl.multiple_of(half * (width // 2), width // 2), width // 2)
    left = lax.broadcasted_iota(jnp.int32, (width // 2, width), 1) < width // 2
    comps = []
    for pair in range(pairs):
        mine = own[pair, rows, :].astype(jnp.float32)
        theirs = other[pair, rows, :].astype(jnp.float32)
        low = jnp.where(half == 0, mine, theirs)
        high = jnp.where(half == 0, theirs, mine)
        comps.append(jnp.where(left, low, pltpu.roll(high, width // 2, 1)))
        comps.append(jnp.where(left, pltpu.roll(low, width // 2, 1), high))
    return jnp.concatenate(comps, axis=0)


def find(tiles, batch, n_row, my_row):
    count = tiles.shape[0] // n_row
    columns = [tiles[batch * count + s] for s in range(count)]
    slot = jnp.int32(0)
    multiple = jnp.int32(0)
    present = jnp.bool_(False)
    for s, tile in enumerate(columns):
        match = lax.rem(tile, n_row) == my_row
        slot = jnp.where(match, s, slot)
        multiple = jnp.where(match, lax.div(tile, n_row), multiple)
        present = jnp.logical_or(present, match)
    owned = [jnp.logical_and(present, owned_multiple(my_row, tile, n_row) == multiple) for tile in columns]
    return columns, slot, multiple, present, owned


def own_rows(basis, batch, slot, half, tile_width, half_tile):
    points = basis.shape[1] * basis.shape[2]
    block = basis[batch, :, :, pl.ds(pl.multiple_of(slot * tile_width, tile_width), tile_width)]
    block = block.reshape(points, tile_width)
    rows = lax.broadcasted_iota(jnp.int32, (half_tile, tile_width), 0) + half * half_tile
    lanes = lax.broadcasted_iota(jnp.int32, (half_tile, tile_width), 1)
    chosen = jnp.where(rows == lanes, 1.0, 0.0).astype(jnp.bfloat16)
    return lax.dot_general(
        chosen, block, (((1,), (1,)), ((), ())), preferred_element_type=jnp.float32
    ).astype(jnp.bfloat16)


def turn_kernel(density, turned, *, n_row, span):
    my_row = lax.axis_index("row")
    my_col = lax.axis_index("col")
    other = 1 - owned_multiple(my_row, my_col, n_row)
    turn(density[pl.ds(pl.multiple_of(other * span, span), span), :], turned)


def symmetric_kernel(density, mine, theirs, total, copies, *, n_row, span):
    my_row = lax.axis_index("row")
    my_col = lax.axis_index("col")
    half = lax.axis_index("grid")
    own = owned_multiple(my_row, my_col, n_row)
    tile = density[pl.ds(pl.multiple_of(own * span, span), span), :].astype(jnp.float32)
    mirror = joined(mine, theirs, half)
    tile = tile + jnp.where(lax.rem(my_col, n_row) == my_row, 0.0, mirror)
    total[...] = tile
    rounded = tile.astype(jnp.bfloat16)
    for dest in range(copies.shape[0]):
        copies[dest] = rounded


def add_densities(tiles, strip, basis, rows_of, weight, screen, out, sums, *, n_col, comps, half_tile, width):
    my_row = lax.axis_index("row")
    n_row, n_half, half_points, functions = basis.shape
    nothing = jnp.zeros(strip.shape[1:], strip.dtype)
    for batch in range(n_row):
        columns, slot, multiple, present, owned = find(tiles, batch, n_row, my_row)
        block = jnp.concatenate(
            [jnp.where(mine, strip[tile], nothing) for tile, mine in zip(columns, owned)], axis=1
        )
        rows = rows_of(batch, slot).astype(jnp.float32)
        samples = basis[batch].reshape(n_half * half_points, functions)
        part = lax.dot_general(block, samples, (((1,), (1,)), ((), ())), preferred_element_type=jnp.float32)
        for comp in range(comps):
            piece = part[comp * half_tile : (comp + 1) * half_tile, :] * rows
            sums[comp, batch : batch + 1, :] = jnp.sum(piece, axis=0, keepdims=True)
    own = weight[...] * screen[...].astype(jnp.float32)
    for dest in range(out.shape[0]):
        h = dest % n_half
        out[dest, 0:comps] = sums[:, :, h * half_points : (h + 1) * half_points]
        if out.shape[1] > comps:
            out[dest, comps] = jnp.broadcast_to(own, out.shape[2:])


def first_density_kernel(tiles, strip, basis_far, weight, screen, out, basis, rows, sums, sems, **sizes):
    half = lax.axis_index("grid")
    groups = sems.shape[0]
    size = basis.shape[0] // groups
    copies = [
        pltpu.make_async_copy(basis_far.at[pl.ds(g * size, size)], basis.at[pl.ds(g * size, size)], sems.at[g])
        for g in range(groups)
    ]
    for copy in copies:
        copy.start()

    def rows_of(batch, slot):
        if batch % size == 0:
            copies[batch // size].wait()
        rows[batch] = own_rows(basis, batch, slot, half, sizes["width"], sizes["half_tile"])
        return rows[batch]

    add_densities(tiles, strip, basis, rows_of, weight, screen, out, sums, **sizes)


def density_kernel(tiles, strip, basis, rows, weight, screen, out, sums, **sizes):
    add_densities(tiles, strip, basis, lambda batch, slot: rows[batch], weight, screen, out, sums, **sizes)


def scales_of(dens, weights):
    total = dens[0]
    spin = [dens[comp] for comp in range(1, dens.shape[0])]
    norm = jnp.sqrt(1.0 + sum(s * s for s in spin))
    potentials = [total / jnp.sqrt(1.0 + total * total)] + [s / norm for s in spin]
    return [potential * weights for potential in potentials]


def first_scale_kernel(arrived, scales, weights):
    comps = scales.shape[0]
    n_row = weights.shape[0]
    half = lax.axis_index("grid")
    n_half = arrived.shape[0] // n_row
    for q in range(n_row):
        weights[q : q + 1, :] = arrived[q * n_half + half, comps, 0:1, :]
    for comp, scale in enumerate(scales_of(jnp.sum(arrived[:, 0:comps], axis=0), weights[...])):
        scales[comp] = scale


def scale_kernel(arrived, weights, scales):
    for comp, scale in enumerate(scales_of(jnp.sum(arrived[...], axis=0), weights[...])):
        scales[comp] = scale


def potential_kernel(tiles, own, other, basis, rows, out, scales, acc, *, n_col, comps, half_tile, width):
    my_row = lax.axis_index("row")
    half = lax.axis_index("grid")
    n_row, n_half, half_points, functions = basis.shape
    multiples = out.shape[1]
    acc[...] = jnp.zeros_like(acc)
    scales[:, :, pl.ds(pl.multiple_of(half * half_points, half_points), half_points)] = own[...]
    scales[:, :, pl.ds(pl.multiple_of((1 - half) * half_points, half_points), half_points)] = other[...]
    for batch in range(n_row):
        columns, slot, multiple, present, owned = find(tiles, batch, n_row, my_row)
        samples = basis[batch].reshape(n_half * half_points, functions)
        factor = rows[batch].astype(jnp.float32)
        weighted = jnp.concatenate(
            [(factor * scales[comp, batch : batch + 1, :]).astype(jnp.bfloat16) for comp in range(comps)], axis=0
        )
        part = jnp.dot(weighted, samples, preferred_element_type=jnp.float32)
        m = 0 if multiples == 1 else multiple
        for s, tile in enumerate(columns):
            mine = owned[s] if multiples == 1 else present
            tile = jnp.where(mine, tile, n_col)
            acc[tile, m] += part[:, s * width : (s + 1) * width]
    out[...] = acc[0:n_col].astype(jnp.bfloat16)


def update_kernel(pieces, density, first, turned, copies, *, n_row):
    my_row = lax.axis_index("row")
    my_col = lax.axis_index("col")
    total = jnp.sum(pieces[...].astype(jnp.float32), axis=(0, 1)).astype(jnp.bfloat16)
    first[...] = total
    mixing = jnp.where(lax.rem(my_col, n_row) == my_row, MIXING, 2.0 * MIXING)
    updated = (density[...] + mixing * total.astype(jnp.float32)).astype(jnp.bfloat16)
    for dest in range(copies.shape[0]):
        copies[dest] = updated
    turn(total, turned)


def mirror_kernel(first, mine, theirs, first_out, *, n_row):
    my_row = lax.axis_index("row")
    my_col = lax.axis_index("col")
    half = lax.axis_index("grid")
    own = owned_multiple(my_row, my_col, n_row)
    unpaired = lax.rem(my_col, n_row) == my_row
    first_out[own] = first[...]
    first_out[1 - own] = jnp.where(unpaired, 0.0, joined(mine, theirs, half)).astype(jnp.bfloat16)


def sum_kernel(pieces, out):
    out[...] = jnp.sum(pieces[...].astype(jnp.float32), axis=0).astype(jnp.bfloat16)


def body(density, basis_values, quad_weight, screen, tile_list):
    n_row = lax.axis_size("row")
    n_col = lax.axis_size("col")
    n_grid = lax.axis_size("grid")
    row_tiles, _, comps, half_tile, width = density.shape
    half_points, functions = basis_values.shape[1:]
    points = half_points * n_grid
    rows = row_tiles * comps * half_tile
    span = comps * half_tile
    sizes = dict(n_col=n_col, comps=comps, half_tile=half_tile, width=width)
    own = density.reshape(rows, width)
    everywhere = ("row", "col", "grid")
    bf16 = lambda *shape: jax.ShapeDtypeStruct(shape, jnp.bfloat16)
    f32 = lambda *shape: jax.ShapeDtypeStruct(shape, jnp.float32)
    params = pltpu.CompilerParams(vmem_limit_bytes=VMEM_BYTES)
    smem = pl.BlockSpec(memory_space=pltpu.SMEM)
    hbm = pl.BlockSpec(memory_space=pltpu.HBM)
    vmem = pl.BlockSpec(memory_space=pltpu.VMEM)
    near = lambda x: pltpu.with_memory_space_constraint(x, pltpu.VMEM)

    def call(kernel, ins, outs, scratch=(), **settings):
        return pl.pallas_call(
            functools.partial(kernel, **settings),
            in_specs=ins,
            out_specs=[vmem] * len(outs),
            out_shape=outs,
            scratch_shapes=list(scratch),
            compiler_params=params,
        )

    block = (comps // n_grid, width, width)
    swap = [(0, 1), (1, 0)]
    sums = pltpu.VMEM((comps, n_row, points), jnp.float32)
    basis_shape = (n_row, n_grid, half_points, functions)
    basis_far = lax.all_gather(basis_values, ("row", "grid"), axis=0, tiled=True).reshape(basis_shape)

    def exchange(turned, back):
        mine = lax.ppermute(turned, everywhere, exchanges(n_row, n_col, n_grid, back))
        return mine, lax.ppermute(mine, "grid", swap)

    by_row = tile_list.reshape(n_row, n_col, tile_list.shape[1])
    tiles = lax.dynamic_index_in_dim(by_row, lax.axis_index("col"), 1, keepdims=False).reshape(-1)
    [turned] = call(turn_kernel, [vmem], [bf16(*block)], n_row=n_row, span=span)(own)
    symmetric, copies = call(
        symmetric_kernel, [vmem] * 3, [f32(span, width), bf16(n_col, span, width)], n_row=n_row, span=span
    )(own, *exchange(turned, True))

    def summed(partial):
        return near(lax.all_to_all(partial, ("row", "grid"), 0, 0, tiled=True))

    def slabs(mine, basis, multiples):
        other = lax.ppermute(mine, "grid", swap)
        shape = (n_col, multiples, span, width)
        [slab] = call(
            potential_kernel,
            [smem] + [vmem] * 4,
            [bf16(*shape)],
            [sums, pltpu.VMEM((n_col + 1, *shape[1:]), jnp.float32)],
            **sizes,
        )(tiles, near(mine), other, basis, kept_rows)
        return lax.all_to_all(slab, "col", 0, 0, tiled=True)

    message = (n_row * n_grid, comps, n_row, half_points)
    strip = near(lax.all_to_all(copies, "col", 0, 0, tiled=True))
    partial, basis, kept_rows = call(
        first_density_kernel,
        [smem, vmem, hbm, vmem, vmem],
        [f32(message[0], comps + 1, *message[2:]), bf16(*basis_shape), bf16(n_row, half_tile, points)],
        [sums, pltpu.SemaphoreType.DMA((2,))],
        **sizes,
    )(tiles, strip, pltpu.with_memory_space_constraint(basis_far, pltpu.HBM), quad_weight, screen)
    basis, kept_rows = near(basis), near(kept_rows)
    mine, weights = call(first_scale_kernel, [vmem], [f32(*message[1:]), f32(*message[2:])])(summed(partial))
    first, turned, copies = call(
        update_kernel, [vmem] * 2, [bf16(span, width), bf16(*block), bf16(n_col, span, width)], n_row=n_row
    )(slabs(mine, basis, 1), symmetric)
    mirrors = exchange(turned, False)
    strip = near(lax.all_to_all(copies, "col", 0, 0, tiled=True))
    [partial] = call(density_kernel, [smem] + [vmem] * 5, [f32(*message)], [sums], **sizes)(
        tiles, strip, basis, kept_rows, quad_weight, screen
    )
    [mine] = call(scale_kernel, [vmem] * 2, [f32(*message[1:])])(summed(partial), near(weights))
    whole = [bf16(row_tiles, span, width)]
    outs = call(mirror_kernel, [vmem] * 3, whole, n_row=n_row)(first, *mirrors)
    outs += call(sum_kernel, [vmem], whole)(slabs(mine, basis, row_tiles))
    return tuple(out.reshape(density.shape) for out in outs)


def solution(mesh):
    in_specs = (
        P(None, "row", None, "grid", "col"),
        P(("row", "col"), "grid", None),
        P(("row", "col"), "grid"),
        P(("row", "col"), "grid"),
        P(),
    )
    out_specs = (P(None, "row", None, "grid", "col"), P(None, "row", None, "grid", "col"))
    return jax.shard_map(body, mesh=mesh, in_specs=in_specs, out_specs=out_specs, check_vma=False)
```
